32 devices in a mesh: ctx: 8 (over z, y), pack: 4 (over x, core).
Axes of the slice: x: 2, y: 2, z: 4, core: 2. Of those that a mesh axis runs over, the one named last changes fastest.
Arguments:
- hidden: bfloat16 [8192, 2048], P(('ctx', 'pack')), may hold values from -4 to 4
- first_keys: bfloat16 [8192, 2048], P('ctx', 'pack'), may hold values from -400 to 400
- first_values: bfloat16 [8192, 2048], P('ctx', 'pack'), may hold values from -18 to 18
- w_query: bfloat16 [2048, 2048], P(None, 'pack'), may hold values from -0.125 to 0.125
- w_out: bfloat16 [2048, 2048], P('pack'), may hold values from -0.125 to 0.125
- norm_gain: float32 [2048], replicated, may hold values from 0.1 to 1.9
- router_weight: float32 [2048], replicated, may hold values from -0.5 to 0.5
- route_list: int32 [8, 256], P('ctx'), may hold values from 0 to 1023, as said below
- pack_order: int32 [8, 256], P('ctx'), may hold values from 0 to 255, each once within a row
- pattern: int32 [8, 12], replicated, may hold values from 0 to 7
Outputs:
- hidden_out: bfloat16 [8192, 2048], P(('ctx', 'pack'))
- packed_states: bfloat16 [2048, 2048], P(('ctx', 'pack'))
The draws below stay inside these ranges and needn't reach their ends.
Inputs may be any that keep to these rules, and one draw needn't show every extreme that they name: `route_list`: each row lists 256 distinct span-local positions in ascending order. At most 96 of a row's positions lie among the 256 tokens of one device, and in every row some device holds exactly 96.
All inputs are finite; a program needn't handle non-finite values.
Results may differ from the reference program's by a relative error of at most 0.023.
Values may be sent and summed in bfloat16 or wider, within the bound.
No kernel may reach another device: no remote copies, remote signals or barrier semaphores. Data moves between devices by JAX's collectives and lax.ppermute only.
A program may use at most 128 MiB of HBM per device.

```python
import math
import jax
import jax.numpy as jnp
from jax import lax

D = 2048
HEADS = 16
HD = 128
NSEL = 12
TOK_DEV = 256
CH = 1024
SEQ = 8192
Q_CH = 256
N_CTX = 8
N_PACK = 4


def draw_route_list(key, part):
    key_counts = jax.random.fold_in(key, 101)
    key_top = jax.random.fold_in(key, 202)
    key_pick = jax.random.fold_in(key, 303)
    shifts = jax.random.randint(key_counts, (N_CTX, N_PACK), 0, TOK_DEV // 8 + 1)
    top_lane = jax.random.randint(key_top, (N_CTX, 1), 0, N_PACK)
    lane_ids = jnp.arange(N_PACK, dtype=jnp.int32)[None, :]
    shifts = jnp.where(lane_ids == top_lane, TOK_DEV // 8, jnp.where(lane_ids == (top_lane + 1) % N_PACK, 0, shifts))
    counts = TOK_DEV // 4 + shifts - jnp.roll(shifts, -1, axis=1)
    scores = jax.random.randint(key_pick, (N_CTX, N_PACK, TOK_DEV), 0, 1 << 20) * TOK_DEV + jnp.arange(TOK_DEV, dtype=jnp.int32)[None, None, :]
    ranks = jnp.argsort(jnp.argsort(scores, axis=-1), axis=-1)
    chosen = (ranks < counts[:, :, None]).reshape(N_CTX, CH)
    sort_keys = jnp.where(chosen, 0, CH) + jnp.arange(CH, dtype=jnp.int32)[None, :]
    listed = jnp.argsort(sort_keys, axis=1)[:, :Q_CH]
    return listed.astype(jnp.int32)


def draw_first_keys(key, part):
    base = jax.random.normal(key, (SEQ, D), jnp.float32)
    drawn = jnp.clip(base, -6.0, 6.0) * 2.0
    return drawn.astype(jnp.bfloat16)


def plant(array, stream_key, low, high):
    dims = array.shape
    spot = [jax.random.randint(jax.random.fold_in(stream_key, axis), (), 0, dims[axis]) for axis in range(len(dims))]
    array = array.at[tuple(spot)].set(low)
    longest = dims.index(max(dims))
    spot[longest] = (spot[longest] + 1) % dims[longest]
    return array.at[tuple(spot)].set(high)


def shard_levels(rng, shape, split, least, top_value):
    def one(axis_at, parts):
        steps = jax.random.uniform(jax.random.fold_in(jax.random.fold_in(rng, 6), axis_at), (parts,), jnp.float32, least / len(split), top_value / len(split))
        return jnp.repeat(jnp.exp(steps), shape[axis_at] // parts).reshape((-1,) + (1,) * (len(shape) - axis_at - 1))

    loudness = one(*split[0])
    for cut in split[1:]:
        loudness = loudness * one(*cut)
    return loudness


def scatter_about(stream_key, extent, deviation, reach, shards=(), kind=jnp.bfloat16):
    loudness = shard_levels(stream_key, extent, shards, -0.22, 0.18) if shards else 1.0
    entries = jax.random.normal(stream_key, extent, jnp.float32) * deviation * loudness
    return jnp.minimum(jnp.maximum(entries, -reach), reach).astype(kind)


def setup_inputs(seed: int = 0) -> dict:
    seeds = jax.random.split(jax.random.key(seed), 11)
    return {
        "hidden": scatter_about(seeds[0], (SEQ, D), 0.25, 4.0, ((0, 32),)),
        "first_keys": draw_first_keys(jax.random.fold_in(seeds[10], 71), 0),
        "first_values": scatter_about(seeds[2], (SEQ, D), 3.0, 18.0, ((0, 8), (1, 4))),
        "w_query": scatter_about(seeds[3], (D, D), D ** -0.5, 0.125, ((1, 4),)),
        "w_out": scatter_about(seeds[4], (D, D), D ** -0.5, 0.125, ((0, 4),)),
        "norm_gain": jnp.clip(1.0 + 0.18 * jax.random.normal(seeds[5], (D,), jnp.float32), 0.1, 1.9),
        "router_weight": scatter_about(seeds[6], (D,), (D // 16) ** -0.5, 0.5, (), jnp.float32),
        "route_list": draw_route_list(jax.random.fold_in(seeds[10], 71), 0),
        "pack_order": jax.vmap(lambda own: jax.random.permutation(own, Q_CH))(jax.random.split(seeds[8], N_CTX)).reshape((N_CTX, Q_CH)).astype(jnp.int32),
        "pattern": plant(jax.random.randint(seeds[9], (N_CTX, NSEL), 0, N_CTX), jax.random.fold_in(seeds[9], 1), 0, N_CTX - 1).astype(jnp.int32),
    }


epsilon = 1e-06
very_negative = -1e+30

def rotate(projected, position, head_count):
    row_count = projected.shape[0]
    head_size = projected.shape[1] // head_count
    half_size = head_size // 2
    frequency = 10000.0 ** (-jnp.arange(half_size, dtype=jnp.float32) * 2.0 / head_size)
    angle = position.astype(jnp.float32)[:, None] * frequency[None, :]
    cosine = jnp.cos(angle)[:, None, :]
    sine_part = jnp.sin(angle)[:, None, :]
    shaped = projected.reshape(row_count, head_count, head_size)
    front_half = shaped[..., :half_size]
    back_half = shaped[..., half_size:]
    turned = jnp.concatenate([front_half * cosine - back_half * sine_part, back_half * cosine + front_half * sine_part], axis=-1)
    return turned.reshape(row_count, head_count * head_size)

def partial_block(query_heads, key_heads, value_heads, allowed):
    scale_factor = 1.0 / math.sqrt(query_heads.shape[2])
    scores = jnp.einsum('qhd,khd->hqk', query_heads.astype(jnp.float32), key_heads.astype(jnp.float32)) * scale_factor
    if allowed is not None:
        scores = jnp.where(allowed[None], scores, very_negative)
    row_peak = lax.optimization_barrier(jnp.max(scores, axis=-1))
    weights = jnp.exp(scores - row_peak[..., None])
    if allowed is not None:
        weights = jnp.where(allowed[None], weights, 0.0)
    weight_sum = lax.optimization_barrier(jnp.sum(weights, axis=-1))
    rounded = weights.astype(jnp.bfloat16)
    summed = jnp.einsum('hqk,khd->qhd', rounded.astype(jnp.float32), value_heads.astype(jnp.float32))
    return (row_peak, weight_sum, summed)

def merge(former, latter):
    new_peak = jnp.maximum(former[0], latter[0])
    former_scale = jnp.exp(former[0] - new_peak)
    latter_scale = jnp.exp(latter[0] - new_peak)
    weight_sum = former_scale * former[1] + latter_scale * latter[1]
    summed = jnp.transpose(former_scale)[:, :, None] * former[2] + jnp.transpose(latter_scale)[:, :, None] * latter[2]
    return (new_peak, weight_sum, summed)

def reference(hidden, first_keys, first_values, w_query, w_out, norm_gain, router_weight, route_list, pack_order, pattern):
    picked = jnp.take_along_axis(route_list, pack_order, axis=1)
    position = (picked + (jnp.arange(N_CTX, dtype=jnp.int32) * CH)[:, None]).reshape(-1).astype(jnp.int32)
    routed_rows = hidden[position]
    rows_float = routed_rows.astype(jnp.float32)
    gate_value = jax.nn.sigmoid(jnp.dot(rows_float, router_weight, precision=lax.Precision.HIGHEST))
    mean_square = lax.optimization_barrier(jnp.mean(rows_float * rows_float, axis=-1, keepdims=True))
    normed = (rows_float * lax.rsqrt(mean_square + epsilon) * norm_gain).astype(jnp.bfloat16)
    queries = rotate(jnp.dot(normed, w_query, preferred_element_type=jnp.float32), position, HEADS).astype(jnp.bfloat16)

    def one_span(span_idx):
        query_heads = lax.dynamic_slice_in_dim(queries, span_idx * Q_CH, Q_CH, 0).reshape(Q_CH, HEADS, HD)
        query_pos = lax.dynamic_slice_in_dim(position, span_idx * Q_CH, Q_CH, 0)
        own_keys = lax.dynamic_slice_in_dim(first_keys, span_idx * CH, CH, 0).reshape(CH, HEADS, HD)
        own_values = lax.dynamic_slice_in_dim(first_values, span_idx * CH, CH, 0).reshape(CH, HEADS, HD)
        key_pos = span_idx * CH + jnp.arange(CH, dtype=jnp.int32)
        running = partial_block(query_heads, own_keys, own_values, key_pos[None, :] <= query_pos[:, None])
        wanted = pattern[span_idx]

        def visit(block_idx, held):
            block_idx = block_idx.astype(jnp.int32)
            active = jnp.logical_and(block_idx < span_idx, jnp.any(wanted == block_idx))

            def take(inner):
                key_block = lax.dynamic_slice_in_dim(first_keys, block_idx * CH, CH, 0).reshape(CH, HEADS, HD)
                value_block = lax.dynamic_slice_in_dim(first_values, block_idx * CH, CH, 0).reshape(CH, HEADS, HD)
                return merge(inner, partial_block(query_heads, key_block, value_block, None))
            return lax.cond(active, take, lambda inner: inner, held)
        running = lax.fori_loop(jnp.int32(0), jnp.int32(N_CTX), visit, running)
        attended = running[2] / jnp.transpose(running[1])[:, :, None]
        return attended.reshape(Q_CH, D).astype(jnp.bfloat16)
    attended = lax.map(one_span, jnp.arange(N_CTX, dtype=jnp.int32)).reshape(N_CTX * Q_CH, D)
    mixed = jnp.dot(attended, w_out, preferred_element_type=jnp.float32)
    packed_states = (rows_float + gate_value[:, None] * mixed).astype(jnp.bfloat16)
    hidden_out = hidden.at[position].set(packed_states)
    return (hidden_out, packed_states)
```

```python
import functools
import math

import jax
import jax.numpy as jnp
from jax import lax
from jax.experimental import pallas as pl
from jax.experimental.pallas import tpu as pltpu
from jax.sharding import PartitionSpec as P

HD = 128
EPS = 1e-06
NEG = -1e30
TAIL = 32
SCALE = math.log2(math.e) / math.sqrt(HD)


def contract(left, right, left_dim, right_dim):
    return lax.dot_general(
        left, right, (((left_dim,), (right_dim,)), ((), ())), preferred_element_type=jnp.float32
    )


def run(body, *, grid, scalars, in_specs, out_specs, out_shape, scratch=(), cost=None, name=None):
    return pl.pallas_call(
        body,
        grid_spec=pltpu.PrefetchScalarGridSpec(
            num_scalar_prefetch=scalars,
            grid=grid,
            in_specs=in_specs,
            out_specs=out_specs,
            scratch_shapes=list(scratch),
        ),
        out_shape=out_shape,
        cost_estimate=cost,
        name=name,
    )


def cost_of(flops, moved, exps=0):
    return pl.CostEstimate(flops=int(flops), bytes_accessed=int(moved), transcendentals=int(exps))


def pick_body(ids, routes_ref, hidden_ref, out_ref):
    tok = hidden_ref.shape[0]
    cap = out_ref.shape[0]
    routed = routes_ref.shape[0]
    base = ids[1] * tok
    routes = routes_ref[...]
    start = jnp.sum(jnp.where(routes < base, 1.0, 0.0), axis=0, keepdims=True).astype(jnp.int32)
    token = lax.broadcasted_iota(jnp.int32, (routed, tok), 1) + base
    hit = jnp.where(routes == token, 1.0, 0.0).astype(jnp.bfloat16)
    entry = lax.broadcasted_iota(jnp.int32, (cap, routed), 1)
    slot = lax.broadcasted_iota(jnp.int32, (cap, routed), 0)
    choose = jnp.where(entry == slot + start, 1.0, 0.0).astype(jnp.bfloat16)
    one_hot = contract(choose, hit, 1, 0).astype(jnp.bfloat16)
    out_ref[...] = contract(one_hot, hidden_ref[...], 1, 0).astype(out_ref.dtype)


def query_body(xors, tok, ids, *refs):
    count = len(xors)
    pieces = refs[:count]
    routes_ref, order_ref, gain_ref, router_ref, cos_ref, sin_ref, wq_ref = refs[count : count + 7]
    rows_ref, gate_ref, query_ref = refs[count + 7 :]
    cap = pieces[0].shape[0]
    routed = order_ref.shape[0]
    routes = routes_ref[...]
    order = order_ref[...]
    entry = lax.broadcasted_iota(jnp.int32, (routed, cap), 1)
    rows = None
    for xor, piece in zip(xors, pieces):
        owner = ids[1] ^ xor
        start = jnp.sum(
            jnp.where(routes < owner * tok, 1.0, 0.0), axis=1, keepdims=True
        ).astype(jnp.int32)
        stop = jnp.sum(
            jnp.where(routes < (owner + 1) * tok, 1.0, 0.0), axis=1, keepdims=True
        ).astype(jnp.int32)
        listed = entry + start
        one_hot = jnp.where((order == listed) & (listed < stop), 1.0, 0.0).astype(jnp.bfloat16)
        term = contract(one_hot, piece[...], 1, 0)
        rows = term if rows is None else rows + term
    rows_ref[...] = rows.astype(rows_ref.dtype)
    logit = jnp.sum(rows * router_ref[...], axis=1, keepdims=True)
    gate_ref[...] = jnp.broadcast_to(1.0 / (1.0 + jnp.exp(-logit)), gate_ref.shape)
    mean_square = jnp.mean(rows * rows, axis=1, keepdims=True)
    normed = (rows * lax.rsqrt(mean_square + EPS) * gain_ref[...]).astype(jnp.bfloat16)
    projected = contract(normed, wq_ref[...], 1, 0)
    cosine = cos_ref[...]
    sine = sin_ref[...]
    for head in range(query_ref.shape[1] // HD):
        part = projected[:, head * HD : (head + 1) * HD]
        turned = part * cosine + pltpu.roll(part, HD // 2, 1) * sine
        query_ref[:, head * HD : (head + 1) * HD] = turned.astype(query_ref.dtype)


def attend_body(shift, n_ctx, chunk, ids, pattern, *refs):
    if shift == 0:
        qpos_ref, refs = refs[0], refs[1:]
    q_ref, k_own, v_own, k_oth, v_oth, out_ref, m_ref, l_ref, acc_ref, log_ref = refs
    head = pl.program_id(1)
    span = k_own.shape[0]
    width = out_ref.shape[0] - TAIL
    here = ids[0]
    source = here + 2 * shift
    other = here ^ 1
    row = jnp.minimum(source, n_ctx - 1)
    has_own = pattern[row, 0] == here
    has_other = pattern[row, 0] == other
    for at in range(1, pattern.shape[1]):
        has_own = has_own | (pattern[row, at] == here)
        has_other = has_other | (pattern[row, at] == other)
    inside = source < n_ctx

    m_ref[...] = jnp.full_like(m_ref, NEG)
    l_ref[...] = jnp.zeros_like(l_ref)
    acc_ref[...] = jnp.zeros_like(acc_ref)

    def block(k_ref, v_ref, masked):
        for at in range(0, span, chunk):
            scores = contract(k_ref[at : at + chunk, :], q_ref[...], 1, 1) * SCALE
            if masked:
                kpos = lax.broadcasted_iota(jnp.int32, scores.shape, 0) + at
                scores = jnp.where(kpos <= qpos_ref[...], scores, NEG)
            former = m_ref[...]
            peak = jnp.maximum(former, jnp.max(scores, axis=0, keepdims=True))
            if masked and at > 0:
                weights = jnp.where(kpos <= qpos_ref[...], jnp.exp2(scores - peak), 0.0)
            else:
                weights = jnp.exp2(scores - peak)
            fade = jnp.exp2(former - peak)
            m_ref[...] = peak
            l_ref[...] = l_ref[...] * fade + jnp.sum(weights, axis=0, keepdims=True)
            acc_ref[...] = acc_ref[...] * fade + contract(
                v_ref[at : at + chunk, :], weights.astype(jnp.bfloat16), 0, 0
            )

    if shift == 0:
        block(k_own, v_own, True)
    else:
        pl.when(inside & has_own)(lambda: block(k_own, v_own, False))
    pl.when(inside & has_other & (other < source))(lambda: block(k_oth, v_oth, False))

    total = l_ref[...]
    some = total > 0.0
    safe = jnp.where(some, total, 1.0)
    out_ref[pl.ds(pl.multiple_of(head * HD, HD), HD), :] = (acc_ref[...] / safe).astype(
        out_ref.dtype
    )
    log_ref[pl.ds(head, 1), :] = jnp.where(some, m_ref[...] + jnp.log2(safe), NEG)

    @pl.when(head == pl.num_programs(1) - 1)
    def _():
        level = log_ref[...]
        high = level.astype(jnp.bfloat16).astype(jnp.float32)
        rest = level - high
        middle = rest.astype(jnp.bfloat16).astype(jnp.float32)
        low = rest - middle
        out_ref[width:, :] = jnp.concatenate(
            [high, middle, low, jnp.zeros_like(low)], axis=0
        ).astype(out_ref.dtype)


def merge_body(shifts, ids, *refs):
    parts, out_ref = refs[:-1], refs[-1]
    width = out_ref.shape[0]
    levels = []
    for shift, part in zip(shifts, parts):
        tail = part[width:, :].astype(jnp.float32)
        level = tail[0:8] + tail[8:16] + tail[16:24]
        if shift:
            level = jnp.where(ids[0] >= 2 * shift, level, NEG)
        levels.append(level)
    peak = functools.reduce(jnp.maximum, levels)
    weights = [jnp.exp2(level - peak) for level in levels]
    inverse = 1.0 / functools.reduce(lambda a, b: a + b, weights)
    for head in range(width // HD):
        cut = slice(head * HD, (head + 1) * HD)
        total = None
        for weight, part in zip(weights, parts):
            term = part[cut, :].astype(jnp.float32) * (weight * inverse)[head : head + 1, :]
            total = term if total is None else total + term
        out_ref[cut, :] = total.astype(out_ref.dtype)


def finish_body(count, ids, *refs):
    attended = refs[:count]
    weights = refs[count : 2 * count]
    rows_ref, gate_ref, picked_ref, hidden_ref = refs[2 * count : 2 * count + 4]
    hidden_out, packed_out, flat_ref, place_ref, new_ref = refs[2 * count + 4 :]
    tok = hidden_ref.shape[0]
    routed = rows_ref.shape[0]
    own = packed_out.shape[0]
    part = attended[0].shape[0]

    @pl.when(pl.program_id(0) == 0)
    def _():
        for at in range(count):
            flat_ref[:, at * part : (at + 1) * part] = jnp.transpose(attended[at][...])
        token = lax.broadcasted_iota(jnp.int32, (tok, routed), 0) + ids[1] * tok
        place_ref[...] = jnp.where(picked_ref[...] == token, 1.0, 0.0).astype(place_ref.dtype)

    mixed = None
    for at in range(count):
        term = contract(flat_ref[:, at * part : (at + 1) * part], weights[at][...], 1, 0)
        mixed = term if mixed is None else mixed + term
    new = rows_ref[...].astype(jnp.float32) + gate_ref[:, 0:1] * mixed
    new_ref[...] = new.astype(new_ref.dtype)
    packed_out[...] = new_ref[pl.ds(pl.multiple_of(ids[1] * own, own), own), :]
    place = place_ref[...]
    moved = contract(place, new_ref[...], 1, 0)
    filled = jnp.sum(place.astype(jnp.float32), axis=1, keepdims=True) > 0.0
    hidden_out[...] = jnp.where(filled, moved, hidden_ref[...].astype(jnp.float32)).astype(
        hidden_out.dtype
    )


def exchange(pieces, n_pack, bit):
    perm = [(p, p ^ bit) for p in range(n_pack)]
    return [lax.ppermute(piece, "pack", perm) for piece in pieces]


def gather_pack(piece, n_pack):
    pieces, xors = [piece], [0]
    bit = n_pack // 2
    while bit:
        pieces = pieces + exchange(pieces, n_pack, bit)
        xors = xors + [x ^ bit for x in xors]
        bit //= 2
    return pieces, xors


def local(
    hidden,
    first_keys,
    first_values,
    w_query,
    w_out,
    norm_gain,
    router_weight,
    route_list,
    pack_order,
    pattern,
):
    n_ctx = lax.axis_size("ctx")
    n_pack = lax.axis_size("pack")
    ctx = lax.axis_index("ctx")
    pack = lax.axis_index("pack")
    tok, width = hidden.shape
    span, part = first_keys.shape
    heads = part // HD
    routed = route_list.shape[1]
    own = routed // n_pack
    cap = 3 * tok // 8
    ids = jnp.stack([ctx, pack]).astype(jnp.int32)
    whole = lambda shape: pl.BlockSpec(shape, lambda *_: (0,) * len(shape))
    bf16, f32 = jnp.bfloat16, jnp.float32

    outgoing = run(
        pick_body,
        grid=(1,),
        scalars=1,
        in_specs=[whole((routed, 1)), whole((tok, width))],
        out_specs=whole((cap, width)),
        out_shape=jax.ShapeDtypeStruct((cap, width), bf16),
        cost=cost_of(2 * cap * tok * width, 2 * tok * width * 2),
        name="pick",
    )(ids, route_list.reshape(routed, 1), hidden)

    pieces, xors = gather_pack(outgoing, n_pack)

    swap = [(c, c ^ 1) for c in range(n_ctx)]
    keys_in, values_in, _ = lax.optimization_barrier((first_keys, first_values, outgoing))
    other_keys = lax.ppermute(keys_in, "ctx", swap)
    other_values = lax.ppermute(values_in, "ctx", swap)

    picked = jnp.sum(
        jnp.where(
            pack_order[0][:, None] == jnp.arange(routed, dtype=jnp.int32)[None, :],
            route_list[0][None, :],
            0,
        ),
        axis=1,
    )
    position = picked + ctx * span
    half = HD // 2
    frequency = 10000.0 ** (-jnp.arange(half, dtype=f32) * 2.0 / HD)
    angle = position.astype(f32)[:, None] * frequency[None, :]
    cosine, sine = jnp.cos(angle), jnp.sin(angle)
    cosine = jnp.concatenate([cosine, cosine], axis=1)
    sine = jnp.concatenate([-sine, sine], axis=1)

    rows, gate, queries = run(
        functools.partial(query_body, xors, tok),
        grid=(1,),
        scalars=1,
        in_specs=[whole((cap, width))] * n_pack
        + [
            whole((1, routed)),
            whole((routed, 1)),
            whole((1, width)),
            whole((1, width)),
            whole((routed, HD)),
            whole((routed, HD)),
            whole((width, part)),
        ],
        out_specs=[whole((routed, width)), whole((routed, HD)), whole((routed, part))],
        out_shape=[
            jax.ShapeDtypeStruct((routed, width), bf16),
            jax.ShapeDtypeStruct((routed, HD), f32),
            jax.ShapeDtypeStruct((routed, part), bf16),
        ],
        cost=cost_of(2 * routed * width * (part + n_pack * cap), 6 * width * part),
        name="query",
    )(
        ids,
        *pieces,
        route_list,
        pack_order.reshape(routed, 1),
        norm_gain.reshape(1, width),
        router_weight.reshape(1, width),
        cosine,
        sine,
        w_query,
    )

    w_in, _ = lax.optimization_barrier((w_out, queries))
    w_pieces, _ = gather_pack(w_in, n_pack)

    q_block = min(routed, 256)
    chunk = min(span, 1024)
    tall = part + TAIL
    pair_flops = 4 * routed * span * part

    def attend(shift, query):
        extra = [pl.BlockSpec((1, q_block), lambda i, h, *_: (0, i))] if shift == 0 else []
        given = [picked.reshape(1, routed)] if shift == 0 else []
        column = lambda i, h, *_: (0, h)
        return run(
            functools.partial(attend_body, shift, n_ctx, chunk),
            grid=(routed // q_block, heads),
            scalars=2,
            in_specs=extra
            + [pl.BlockSpec((q_block, HD), lambda i, h, *_: (i, h))]
            + [pl.BlockSpec((span, HD), column)] * 4,
            out_specs=pl.BlockSpec((tall, q_block), lambda i, h, *_: (0, i)),
            out_shape=jax.ShapeDtypeStruct((tall, routed), bf16),
            scratch=[
                pltpu.VMEM((1, q_block), f32),
                pltpu.VMEM((1, q_block), f32),
                pltpu.VMEM((HD, q_block), f32),
                pltpu.VMEM((8, q_block), f32),
            ],
            cost=cost_of(2 * pair_flops, 4 * span * part * 2, 2 * routed * span * heads),
            name="attend" + str(shift),
        )(ids, pattern, *given, query, first_keys, first_values, other_keys, other_values)

    far = n_ctx // 2 - 1
    moved = {}
    for shift in range(far, 0, -1):
        moved[shift] = lax.ppermute(
            queries, "ctx", [(c, c - 2 * shift) for c in range(2 * shift, n_ctx)]
        )
    parts = []
    for shift in range(far, 0, -1):
        partial = attend(shift, moved[shift])
        parts.append(
            lax.ppermute(partial, "ctx", [(c, c + 2 * shift) for c in range(n_ctx - 2 * shift)])
        )
    parts.append(attend(0, queries))
    shifts = list(range(far, -1, -1))

    attended = run(
        functools.partial(merge_body, shifts),
        grid=(1,),
        scalars=1,
        in_specs=[whole((tall, routed))] * len(parts),
        out_specs=whole((part, routed)),
        out_shape=jax.ShapeDtypeStruct((part, routed), bf16),
        cost=cost_of(8 * routed * part, 2 * tall * routed * len(parts)),
        name="merge",
    )(ids, *parts)

    a_pieces, _ = gather_pack(attended, n_pack)

    columns = width // 4
    slab = lambda rows_: pl.BlockSpec((rows_, columns), lambda j, *_: (0, j))
    hidden_out, packed = run(
        functools.partial(finish_body, n_pack),
        grid=(width // columns,),
        scalars=1,
        in_specs=[whole((part, routed))] * n_pack
        + [slab(part)] * n_pack
        + [slab(routed), whole((routed, HD)), whole((1, routed)), slab(tok)],
        out_specs=[slab(tok), slab(own)],
        out_shape=[
            jax.ShapeDtypeStruct((tok, width), hidden.dtype),
            jax.ShapeDtypeStruct((own, width), hidden.dtype),
        ],
        scratch=[
            pltpu.VMEM((routed, n_pack * part), bf16),
            pltpu.VMEM((tok, routed), bf16),
            pltpu.VMEM((routed, columns), bf16),
        ],
        cost=cost_of(2 * routed * width * width, 2 * width * width),
        name="finish",
    )(ids, *a_pieces, *w_pieces, rows, gate, picked.reshape(1, routed), hidden)
    return (hidden_out, packed)


def solution(mesh):
    return jax.shard_map(
        local,
        mesh=mesh,
        in_specs=(
            P(("ctx", "pack"), None),
            P("ctx", "pack"),
            P("ctx", "pack"),
            P(None, "pack"),
            P("pack", None),
            P(),
            P(),
            P("ctx", None),
            P("ctx", None),
            P(),
        ),
        out_specs=(P(("ctx", "pack"), None), P(("ctx", "pack"), None)),
        check_vma=False,
    )
```

```python
import functools
import math

import jax
import jax.numpy as jnp
from jax import lax
from jax.experimental import pallas as pl
from jax.experimental.pallas import tpu as pltpu
from jax.sharding import PartitionSpec as P


HD = 128
EPS = 1e-06
NEG = -1e30
TAIL = 32
SCALE = math.log2(math.e) / math.sqrt(HD)


def contract(left, right, left_dim, right_dim):
    return lax.dot_general(
        left, right, (((left_dim,), (right_dim,)), ((), ())), preferred_element_type=jnp.float32
    )


def run(body, *, grid, scalars, in_specs, out_specs, out_shape, scratch=(), cost=None, mib=16):
    kernel = call(body, grid, scalars, in_specs, out_specs, out_shape, scratch, cost, mib)

    return kernel


def call(body, grid, scalars, in_specs, out_specs, out_shape, scratch, cost, mib):
    return pl.pallas_call(
        body,
        grid_spec=pltpu.PrefetchScalarGridSpec(
            num_scalar_prefetch=scalars,
            grid=grid,
            in_specs=in_specs,
            out_specs=out_specs,
            scratch_shapes=list(scratch),
        ),
        out_shape=out_shape,
        cost_estimate=cost,
        compiler_params=pltpu.CompilerParams(vmem_limit_bytes=mib * 2**20),
    )


def cost_of(flops, moved, exps=0):
    return pl.CostEstimate(flops=int(flops), bytes_accessed=int(moved), transcendentals=int(exps))


def below(routes, bound):
    return jnp.sum(jnp.where(routes < bound, 1.0, 0.0), axis=1, keepdims=True).astype(jnp.int32)


def pick_body(ids, routes_ref, hidden_ref, out_ref):
    tok = hidden_ref.shape[0]
    cap = out_ref.shape[0]
    routed = routes_ref.shape[1]
    base = ids[1] * tok
    routes = routes_ref[...]
    token = lax.broadcasted_iota(jnp.int32, (tok, routed), 0) + base
    hit = jnp.where(routes == token, 1.0, 0.0).astype(jnp.bfloat16)
    entry = lax.broadcasted_iota(jnp.int32, (cap, routed), 1)
    slot = lax.broadcasted_iota(jnp.int32, (cap, routed), 0)
    choose = jnp.where(entry == slot + below(routes, base), 1.0, 0.0).astype(jnp.bfloat16)
    one_hot = contract(choose, hit, 1, 1).astype(jnp.bfloat16)
    out_ref[...] = contract(one_hot, hidden_ref[...], 1, 0).astype(out_ref.dtype)


def query_body(xors, tok, ids, *refs):
    count = len(xors)
    pieces = refs[:count]
    routes_ref, order_ref, gain_ref, router_ref, cos_ref, sin_ref, wq_ref = refs[count : count + 7]
    rows_ref, gate_ref, query_ref = refs[count + 7 :]
    cap = pieces[0].shape[0]
    routed = order_ref.shape[1]
    routes = routes_ref[...]
    order = order_ref[...]
    entry = lax.broadcasted_iota(jnp.int32, (cap, routed), 0)
    rows = None
    for xor, piece in zip(xors, pieces):
        owner = ids[1] ^ xor
        listed = entry + below(routes, owner * tok)
        stop = below(routes, (owner + 1) * tok)
        one_hot = jnp.where((order == listed) & (listed < stop), 1.0, 0.0).astype(jnp.bfloat16)
        term = contract(one_hot, piece[...], 0, 0)
        rows = term if rows is None else rows + term
    rows_ref[...] = rows.astype(rows_ref.dtype)
    logit = jnp.sum(rows * router_ref[...], axis=1, keepdims=True)
    gate_ref[...] = jnp.broadcast_to(1.0 / (1.0 + jnp.exp(-logit)), gate_ref.shape)
    mean_square = jnp.mean(rows * rows, axis=1, keepdims=True)
    normed = (rows * lax.rsqrt(mean_square + EPS) * gain_ref[...]).astype(jnp.bfloat16)
    projected = contract(normed, wq_ref[...], 1, 0)
    cosine = cos_ref[...]
    sine = sin_ref[...]
    for head in range(query_ref.shape[1] // HD):
        part = projected[:, head * HD : (head + 1) * HD]
        turned = part * cosine + pltpu.roll(part, HD // 2, 1) * sine
        query_ref[:, head * HD : (head + 1) * HD] = turned.astype(query_ref.dtype)


def attend_body(shift, use, n_ctx, chunk, ids, pattern, *refs):
    masked_own = shift == 0 and "own" in use
    if masked_own:
        qpos_ref, refs = refs[0], refs[1:]
    q_ref, refs = refs[0], refs[1:]
    spans = [(refs[2 * i], refs[2 * i + 1]) for i in range(len(use))]
    out_ref, m_ref, l_ref, acc_ref, log_ref = refs[2 * len(use) :]
    head = pl.program_id(1)
    span = spans[0][0].shape[0]
    width = out_ref.shape[0] - TAIL
    here = ids[0]
    source = here + 2 * shift
    row = jnp.minimum(source, n_ctx - 1)

    def attends(key_span):
        found = pattern[row, 0] == key_span
        for at in range(1, pattern.shape[1]):
            found = found | (pattern[row, at] == key_span)
        return found & (source < n_ctx) & (key_span < source)

    m_ref[...] = jnp.full_like(m_ref, NEG)
    l_ref[...] = jnp.zeros_like(l_ref)
    acc_ref[...] = jnp.zeros_like(acc_ref)

    def block(k_ref, v_ref, masked):
        for at in range(0, span, chunk):
            scores = contract(k_ref[at : at + chunk, :], q_ref[...], 1, 1) * SCALE
            if masked:
                kpos = lax.broadcasted_iota(jnp.int32, scores.shape, 0) + at
                scores = jnp.where(kpos <= qpos_ref[...], scores, NEG)
            former = m_ref[...]
            peak = jnp.maximum(former, jnp.max(scores, axis=0, keepdims=True))
            weights = jnp.exp2(scores - peak)
            fade = jnp.exp2(former - peak)
            m_ref[...] = peak
            l_ref[...] = l_ref[...] * fade + jnp.sum(weights, axis=0, keepdims=True)
            acc_ref[...] = acc_ref[...] * fade + contract(
                v_ref[at : at + chunk, :], weights.astype(jnp.bfloat16), 0, 0
            )

    for kind, (k_ref, v_ref) in zip(use, spans):
        if kind == "own" and shift == 0:
            block(k_ref, v_ref, True)
        else:
            key_span = here if kind == "own" else here ^ 1
            pl.when(attends(key_span))(functools.partial(block, k_ref, v_ref, False))

    total = l_ref[...]
    some = total > 0.0
    safe = jnp.where(some, total, 1.0)
    out_ref[pl.ds(pl.multiple_of(head * HD, HD), HD), :] = (acc_ref[...] / safe).astype(
        out_ref.dtype
    )
    log_ref[pl.ds(head, 1), :] = jnp.where(some, m_ref[...] + jnp.log2(safe), NEG)

    @pl.when(head == pl.num_programs(1) - 1)
    def _():
        level = log_ref[...]
        high = level.astype(jnp.bfloat16).astype(jnp.float32)
        rest = level - high
        middle = rest.astype(jnp.bfloat16).astype(jnp.float32)
        low = rest - middle
        out_ref[width:, :] = jnp.concatenate(
            [high, middle, low, jnp.zeros_like(low)], axis=0
        ).astype(out_ref.dtype)


def merge_body(shifts, ids, *refs):
    parts, out_ref = refs[:-1], refs[-1]
    width = out_ref.shape[0]
    levels = []
    for shift, part in zip(shifts, parts):
        tail = part[width:, :].astype(jnp.float32)
        level = tail[0:8] + tail[8:16] + tail[16:24]
        if shift:
            level = jnp.where(ids[0] >= 2 * shift, level, NEG)
        levels.append(level)
    peak = functools.reduce(jnp.maximum, levels)
    weights = [jnp.exp2(level - peak) for level in levels]
    inverse = 1.0 / functools.reduce(lambda a, b: a + b, weights)
    for head in range(width // HD):
        cut = slice(head * HD, (head + 1) * HD)
        total = None
        for weight, part in zip(weights, parts):
            term = part[cut, :].astype(jnp.float32) * (weight * inverse)[head : head + 1, :]
            total = term if total is None else total + term
        out_ref[cut, :] = total.astype(out_ref.dtype)


def finish_body(count, ids, *refs):
    attended = refs[:count]
    weights = refs[count : 2 * count]
    rows_ref, gate_ref, picked_ref, hidden_ref = refs[2 * count : 2 * count + 4]
    hidden_out, packed_out, flat_ref, place_ref, new_ref = refs[2 * count + 4 :]
    tok = hidden_ref.shape[0]
    routed = rows_ref.shape[0]
    own = packed_out.shape[0]
    part = attended[0].shape[0]

    @pl.when(pl.program_id(0) == 0)
    def _():
        for at in range(count):
            flat_ref[:, at * part : (at + 1) * part] = jnp.transpose(attended[at][...])
        token = lax.broadcasted_iota(jnp.int32, (tok, routed), 0) + ids[1] * tok
        place_ref[...] = jnp.where(picked_ref[...] == token, 1.0, 0.0).astype(place_ref.dtype)

    mixed = None
    for at in range(count):
        term = contract(flat_ref[:, at * part : (at + 1) * part], weights[at][...], 1, 0)
        mixed = term if mixed is None else mixed + term
    new = rows_ref[...].astype(jnp.float32) + gate_ref[:, 0:1] * mixed
    new_ref[...] = new.astype(new_ref.dtype)
    packed_out[...] = new_ref[pl.ds(pl.multiple_of(ids[1] * own, own), own), :]
    place = place_ref[...]
    moved = contract(place, new_ref[...], 1, 0)
    filled = jnp.sum(place.astype(jnp.float32), axis=1, keepdims=True) > 0.0
    hidden_out[...] = jnp.where(filled, moved, hidden_ref[...].astype(jnp.float32)).astype(
        hidden_out.dtype
    )


def gather_pack(piece, n_pack):
    pieces, xors = [piece], [0]
    bit = n_pack // 2
    while bit:
        pairs = [(p, p ^ bit) for p in range(n_pack)]
        pieces = pieces + [lax.ppermute(held, "pack", pairs) for held in pieces]
        xors = xors + [x ^ bit for x in xors]
        bit //= 2
    return pieces, xors


def local(
    hidden,
    first_keys,
    first_values,
    w_query,
    w_out,
    norm_gain,
    router_weight,
    route_list,
    pack_order,
    pattern,
):
    n_ctx = lax.axis_size("ctx")
    n_pack = lax.axis_size("pack")
    ctx = lax.axis_index("ctx")
    pack = lax.axis_index("pack")
    tok, width = hidden.shape
    span, part = first_keys.shape
    heads = part // HD
    routed = route_list.shape[1]
    own = routed // n_pack
    cap = 3 * tok // 8
    ids = jnp.stack([ctx, pack]).astype(jnp.int32)
    whole = lambda shape: pl.BlockSpec(shape, lambda *_: (0,) * len(shape))
    bf16, f32 = jnp.bfloat16, jnp.float32

    outgoing = run(
        pick_body,
        grid=(1,),
        scalars=1,
        in_specs=[whole((1, routed)), whole((tok, width))],
        out_specs=whole((cap, width)),
        out_shape=jax.ShapeDtypeStruct((cap, width), bf16),
        cost=cost_of(2 * cap * tok * width, 2 * tok * width * 2),
    )(ids, route_list, hidden)

    pieces, xors = gather_pack(outgoing, n_pack)

    swap = [(c, c ^ 1) for c in range(n_ctx)]
    keys_in, values_in, _ = lax.optimization_barrier((first_keys, first_values, outgoing))
    other_keys = lax.ppermute(keys_in, "ctx", swap)
    other_values = lax.ppermute(values_in, "ctx", swap)

    picked = jnp.sum(
        jnp.where(
            pack_order[0][:, None] == jnp.arange(routed, dtype=jnp.int32)[None, :],
            route_list[0][None, :],
            0,
        ),
        axis=1,
    )
    position = picked + ctx * span
    half = HD // 2
    frequency = 10000.0 ** (-jnp.arange(half, dtype=f32) * 2.0 / HD)
    angle = position.astype(f32)[:, None] * frequency[None, :]
    cosine, sine = jnp.cos(angle), jnp.sin(angle)
    cosine = jnp.concatenate([cosine, cosine], axis=1)
    sine = jnp.concatenate([-sine, sine], axis=1)

    rows, gate, queries = run(
        functools.partial(query_body, xors, tok),
        grid=(1,),
        scalars=1,
        in_specs=[whole((cap, width))] * n_pack
        + [
            whole((1, routed)),
            whole((1, routed)),
            whole((1, width)),
            whole((1, width)),
            whole((routed, HD)),
            whole((routed, HD)),
            whole((width, part)),
        ],
        out_specs=[whole((routed, width)), whole((routed, HD)), whole((routed, part))],
        out_shape=[
            jax.ShapeDtypeStruct((routed, width), bf16),
            jax.ShapeDtypeStruct((routed, HD), f32),
            jax.ShapeDtypeStruct((routed, part), bf16),
        ],
        cost=cost_of(2 * routed * width * (part + n_pack * cap), 6 * width * part),
        mib=32,
    )(
        ids,
        *pieces,
        route_list,
        pack_order,
        norm_gain.reshape(1, width),
        router_weight.reshape(1, width),
        cosine,
        sine,
        w_query,
    )

    w_in, _ = lax.optimization_barrier((w_out, pieces[1]))
    w_pieces, _ = gather_pack(w_in, n_pack)

    q_block = min(routed, 256)
    chunk = min(span, 1024)
    tall = part + TAIL
    pair_flops = 4 * routed * span * part

    def attend(shift, query, use):
        masked = shift == 0 and "own" in use
        extra = [pl.BlockSpec((1, q_block), lambda i, h, *_: (0, i))] if masked else []
        given = [picked.reshape(1, routed)] if masked else []
        column = lambda i, h, *_: (0, h)
        held = {"own": (first_keys, first_values), "other": (other_keys, other_values)}
        arrays = [array for kind in use for array in held[kind]]
        return run(
            functools.partial(attend_body, shift, use, n_ctx, chunk),
            grid=(routed // q_block, heads),
            scalars=2,
            in_specs=extra
            + [pl.BlockSpec((q_block, HD), lambda i, h, *_: (i, h))]
            + [pl.BlockSpec((span, HD), column)] * len(arrays),
            out_specs=pl.BlockSpec((tall, q_block), lambda i, h, *_: (0, i)),
            out_shape=jax.ShapeDtypeStruct((tall, routed), bf16),
            scratch=[
                pltpu.VMEM((1, q_block), f32),
                pltpu.VMEM((1, q_block), f32),
                pltpu.VMEM((HD, q_block), f32),
                pltpu.VMEM((8, q_block), f32),
            ],
            cost=cost_of(len(use) * pair_flops, 4 * span * part * len(use)),
        )(ids, pattern, *given, query, *arrays)

    far = n_ctx // 2 - 1
    moved = {}
    for shift in range(far, 0, -1):
        moved[shift] = lax.ppermute(
            queries, "ctx", [(c, c - 2 * shift) for c in range(2 * shift, n_ctx)]
        )
    parts = [attend(0, queries, ("own",))]
    for shift in range(far, 0, -1):
        partial = attend(shift, moved[shift], ("own", "other"))
        parts.append(
            lax.ppermute(partial, "ctx", [(c, c + 2 * shift) for c in range(n_ctx - 2 * shift)])
        )
    parts.append(attend(0, queries, ("other",)))
    shifts = [0, *range(far, 0, -1), 0]

    attended = run(
        functools.partial(merge_body, shifts),
        grid=(1,),
        scalars=1,
        in_specs=[whole((tall, routed))] * len(parts),
        out_specs=whole((part, routed)),
        out_shape=jax.ShapeDtypeStruct((part, routed), bf16),
        cost=cost_of(8 * routed * part, 2 * tall * routed * len(parts)),
    )(ids, *parts)

    a_pieces, _ = gather_pack(attended, n_pack)

    columns = width // 4
    slab = lambda rows_: pl.BlockSpec((rows_, columns), lambda j, *_: (0, j))
    hidden_out, packed = run(
        functools.partial(finish_body, n_pack),
        grid=(width // columns,),
        scalars=1,
        in_specs=[whole((part, routed))] * n_pack
        + [slab(part)] * n_pack
        + [slab(routed), whole((routed, HD)), whole((1, routed)), slab(tok)],
        out_specs=[slab(tok), slab(own)],
        out_shape=[
            jax.ShapeDtypeStruct((tok, width), hidden.dtype),
            jax.ShapeDtypeStruct((own, width), hidden.dtype),
        ],
        scratch=[
            pltpu.VMEM((routed, n_pack * part), bf16),
            pltpu.VMEM((tok, routed), bf16),
            pltpu.VMEM((routed, columns), bf16),
        ],
        cost=cost_of(2 * routed * width * width, 2 * width * width),
        mib=24,
    )(ids, *a_pieces, *w_pieces, rows, gate, picked.reshape(1, routed), hidden)
    return (hidden_out, packed)


def solution(mesh):
    return jax.shard_map(
        local,
        mesh=mesh,
        in_specs=(
            P(("ctx", "pack"), None),
            P("ctx", "pack"),
            P("ctx", "pack"),
            P(None, "pack"),
            P("pack", None),
            P(),
            P(),
            P("ctx", None),
            P("ctx", None),
            P(),
        ),
        out_specs=(P(("ctx", "pack"), None), P(("ctx", "pack"), None)),
        check_vma=False,
    )
```

```python
import functools
import math

import jax
import jax.numpy as jnp
from jax import lax
from jax.experimental import pallas as pl
from jax.experimental.pallas import tpu as pltpu
from jax.sharding import PartitionSpec as P


HD = 128
EPS = 1e-06
NEG = -1e30
TAIL = 16
GROUPS = 2
SCALE = math.log2(math.e) / math.sqrt(HD)


def contract(left, right, left_dim, right_dim):
    return lax.dot_general(
        left, right, (((left_dim,), (right_dim,)), ((), ())), preferred_element_type=jnp.float32
    )


def run(body, *, grid, scalars, in_specs, out_specs, out_shape, scratch=(), cost=None, mib=16):
    kernel = call(body, grid, scalars, in_specs, out_specs, out_shape, scratch, cost, mib)

    return kernel


def call(body, grid, scalars, in_specs, out_specs, out_shape, scratch, cost, mib):
    return pl.pallas_call(
        body,
        grid_spec=pltpu.PrefetchScalarGridSpec(
            num_scalar_prefetch=scalars,
            grid=grid,
            in_specs=in_specs,
            out_specs=out_specs,
            scratch_shapes=list(scratch),
        ),
        out_shape=out_shape,
        cost_estimate=cost,
        compiler_params=pltpu.CompilerParams(vmem_limit_bytes=mib * 2**20),
    )


def cost_of(flops, moved, exps=0):
    return pl.CostEstimate(flops=int(flops), bytes_accessed=int(moved), transcendentals=int(exps))


def below(routes, bound):
    return jnp.sum(jnp.where(routes < bound, 1.0, 0.0), axis=1, keepdims=True).astype(jnp.int32)


def pick_body(ids, routes_ref, hidden_ref, out_ref):
    tok = hidden_ref.shape[0]
    cap = out_ref.shape[0]
    routed = routes_ref.shape[1]
    base = ids[1] * tok
    routes = routes_ref[...]
    token = lax.broadcasted_iota(jnp.int32, (tok, routed), 0) + base
    hit = jnp.where(routes == token, 1.0, 0.0).astype(jnp.bfloat16)
    entry = lax.broadcasted_iota(jnp.int32, (cap, routed), 1)
    slot = lax.broadcasted_iota(jnp.int32, (cap, routed), 0)
    choose = jnp.where(entry == slot + below(routes, base), 1.0, 0.0).astype(jnp.bfloat16)
    one_hot = contract(choose, hit, 1, 1).astype(jnp.bfloat16)
    out_ref[...] = contract(one_hot, hidden_ref[...], 1, 0).astype(out_ref.dtype)


def query_body(xors, tok, groups, ids, *refs):
    count = len(xors)
    pieces = refs[:count]
    routes_ref, order_ref, gain_ref, router_ref, cos_ref, sin_ref, wq_hbm = refs[count : count + 7]
    rows_ref, gate_ref = refs[count + 7 : count + 9]
    query_refs = refs[count + 9 : count + 9 + groups]
    wq_ref, sem = refs[count + 9 + groups :]
    load = pltpu.make_async_copy(wq_hbm, wq_ref, sem)
    load.start()
    cap = pieces[0].shape[0]
    routed = order_ref.shape[1]
    routes = routes_ref[...]
    order = order_ref[...]
    entry = lax.broadcasted_iota(jnp.int32, (cap, routed), 0)
    rows = None
    for xor, piece in zip(xors, pieces):
        owner = ids[1] ^ xor
        listed = entry + below(routes, owner * tok)
        stop = below(routes, (owner + 1) * tok)
        one_hot = jnp.where((order == listed) & (listed < stop), 1.0, 0.0).astype(jnp.bfloat16)
        term = contract(one_hot, piece[...], 0, 0)
        rows = term if rows is None else rows + term
    rows_ref[...] = rows.astype(rows_ref.dtype)
    logit = jnp.sum(rows * router_ref[...], axis=1, keepdims=True)
    gate_ref[...] = jnp.broadcast_to(1.0 / (1.0 + jnp.exp(-logit)), gate_ref.shape)
    mean_square = jnp.mean(rows * rows, axis=1, keepdims=True)
    normed = (rows * lax.rsqrt(mean_square + EPS) * gain_ref[...]).astype(jnp.bfloat16)
    load.wait()
    projected = contract(normed, wq_ref[...], 1, 0)
    cosine = cos_ref[...]
    sine = sin_ref[...]
    per = query_refs[0].shape[1] // HD
    for head in range(per * groups):
        part = projected[:, head * HD : (head + 1) * HD]
        turned = part * cosine + pltpu.roll(part, HD // 2, 1) * sine
        at = head % per * HD
        query_refs[head // per][:, at : at + HD] = turned.astype(jnp.bfloat16)


def split_body(group, keys_hbm, values_hbm, out_ref, sems):
    span, width = out_ref.shape[0] // 2, out_ref.shape[1]
    loads = [
        pltpu.make_async_copy(
            source.at[:, pl.ds(group * width, width)],
            out_ref.at[pl.ds(at * span, span), :],
            sems.at[at],
        )
        for at, source in enumerate((keys_hbm, values_hbm))
    ]
    for load in loads:
        load.start()
    for load in loads:
        load.wait()


def level_rows(part_ref, heads):
    tail = part_ref[heads * HD :, :].astype(jnp.float32)
    return [
        tail[head : head + 1] + tail[heads + head : heads + head + 1]
        + tail[2 * heads + head : 2 * heads + head + 1]
        for head in range(heads)
    ]


def attend_body(shift, use, prior, n_ctx, ids, pattern, *refs):
    masked_own = shift == 0 and "own" in use
    if masked_own:
        qpos_ref, refs = refs[0], refs[1:]
    if prior:
        prior_ref, refs = refs[0], refs[1:]
    q_ref, refs = refs[0], refs[1:]
    spans, refs = refs[: len(use)], refs[len(use) :]
    out_ref, m_ref, l_ref, acc_ref = refs
    span = spans[0].shape[0] // 2
    chunk = min(span, 1024)
    heads = q_ref.shape[1] // HD
    here = ids[0]
    source = here + 2 * shift
    row = jnp.minimum(source, n_ctx - 1)

    def attends(key_span):
        found = pattern[row, 0] == key_span
        for at in range(1, pattern.shape[1]):
            found = found | (pattern[row, at] == key_span)
        return found & (source < n_ctx) & (key_span < source)

    def block(kv_ref, masked, fresh):
        for at in range(0, span, chunk):
            for head in range(heads):
                cut = slice(head * HD, (head + 1) * HD)
                scores = contract(kv_ref[at : at + chunk, cut], q_ref[:, cut], 1, 1) * SCALE
                if masked:
                    kpos = lax.broadcasted_iota(jnp.int32, scores.shape, 0) + at
                    scores = jnp.where(kpos <= qpos_ref[...], scores, NEG)
                peak = jnp.max(scores, axis=0, keepdims=True)
                if not (fresh and at == 0):
                    former = m_ref[head : head + 1, :]
                    peak = jnp.maximum(former, peak)
                weights = jnp.exp2(scores - peak)
                total = jnp.sum(weights, axis=0, keepdims=True)
                value = contract(
                    kv_ref[span + at : span + at + chunk, cut], weights.astype(jnp.bfloat16), 0, 0
                )
                if not (fresh and at == 0):
                    fade = jnp.exp2(former - peak)
                    total = l_ref[head : head + 1, :] * fade + total
                    value = acc_ref[cut, :] * fade + value
                m_ref[head : head + 1, :] = peak
                l_ref[head : head + 1, :] = total
                acc_ref[cut, :] = value

    if masked_own:
        block(spans[0], True, True)
    else:
        if prior:
            for head, level in enumerate(level_rows(prior_ref, heads)):
                m_ref[head : head + 1, :] = level
                l_ref[head : head + 1, :] = jnp.where(level > 0.5 * NEG, 1.0, 0.0)
            acc_ref[...] = prior_ref[: heads * HD, :].astype(jnp.float32)
        else:
            m_ref[...] = jnp.full_like(m_ref, NEG)
            l_ref[...] = jnp.zeros_like(l_ref)
            acc_ref[...] = jnp.zeros_like(acc_ref)
        for kind, kv_ref in zip(use, spans):
            key_span = here if kind == "own" else here ^ 1
            pl.when(attends(key_span))(functools.partial(block, kv_ref, False, False))

    index = lax.broadcasted_iota(jnp.int32, (TAIL, out_ref.shape[1]), 0)
    tail = jnp.zeros(index.shape, jnp.float32)
    for head in range(heads):
        cut = slice(head * HD, (head + 1) * HD)
        total = l_ref[head : head + 1, :]
        some = total > 0.0
        safe = jnp.where(some, total, 1.0)
        out_ref[cut, :] = (acc_ref[cut, :] * (1.0 / safe)).astype(out_ref.dtype)
        rest = jnp.where(some, m_ref[head : head + 1, :] + jnp.log2(safe), NEG)
        for digit in range(3):
            value = rest.astype(jnp.bfloat16).astype(jnp.float32)
            tail = jnp.where(index == digit * heads + head, value, tail)
            rest = rest - value
    out_ref[heads * HD :, :] = tail.astype(out_ref.dtype)


def merge_body(shifts, ids, *refs):
    parts, out_ref = refs[:-1], refs[-1]
    heads = out_ref.shape[0] // HD
    levels = []
    for shift, part in zip(shifts, parts):
        rows = level_rows(part, heads)
        if shift:
            rows = [jnp.where(ids[0] >= 2 * shift, row, NEG) for row in rows]
        levels.append(rows)
    for head in range(heads):
        cut = slice(head * HD, (head + 1) * HD)
        mine = [rows[head] for rows in levels]
        peak = functools.reduce(jnp.maximum, mine)
        weights = [jnp.exp2(level - peak) for level in mine]
        inverse = 1.0 / functools.reduce(lambda a, b: a + b, weights)
        total = None
        for weight, part in zip(weights, parts):
            term = part[cut, :].astype(jnp.float32) * (weight * inverse)
            total = term if total is None else total + term
        out_ref[cut, :] = total.astype(out_ref.dtype)


def project(attended, weights, offset, columns):
    part = attended[0].shape[0]
    mixed = None
    for rows, weight in zip(attended, weights):
        term = contract(rows[...], weight[offset : offset + part, columns], 0, 0)
        mixed = term if mixed is None else mixed + term
    return mixed


def partial_body(count, offset, prior, *refs):
    attended, weights = refs[:count], refs[count : 2 * count]
    out_ref = refs[-1]
    width = out_ref.shape[1]
    step = min(512, width)
    for at in range(0, width, step):
        columns = slice(at, at + step)
        mixed = project(attended, weights, offset, columns)
        if prior:
            mixed = mixed + refs[2 * count][:, columns]
        out_ref[:, columns] = mixed


def finish_body(count, offset, ids, *refs):
    attended, weights = refs[:count], refs[count : 2 * count]
    sum_ref, rows_ref, gate_ref, picked_ref, hidden_ref = refs[2 * count : 2 * count + 5]
    hidden_out, packed_out, new_ref = refs[2 * count + 5 :]
    tok = hidden_ref.shape[0]
    routed = rows_ref.shape[0]
    own = packed_out.shape[0]
    step = hidden_out.shape[1]
    columns = pl.ds(pl.multiple_of(pl.program_id(0) * step, step), step)
    token = lax.broadcasted_iota(jnp.int32, (tok, routed), 0) + ids[1] * tok
    place = jnp.where(picked_ref[...] == token, 1.0, 0.0)
    filled = jnp.sum(place, axis=1, keepdims=True) > 0.0
    mixed = project(attended, weights, offset, columns) + sum_ref[:, columns]
    new = rows_ref[:, columns].astype(jnp.float32) + gate_ref[:, 0:1] * mixed
    new_ref[...] = new.astype(new_ref.dtype)
    packed_out[...] = new_ref[pl.ds(pl.multiple_of(ids[1] * own, own), own), :]
    moved = contract(place.astype(jnp.bfloat16), new_ref[...], 1, 0)
    hidden_out[...] = jnp.where(
        filled, moved, hidden_ref[:, columns].astype(jnp.float32)
    ).astype(hidden_out.dtype)


def gather_pack(piece, n_pack):
    pieces, xors = [piece], [0]
    bit = n_pack // 2
    while bit:
        pairs = [(p, p ^ bit) for p in range(n_pack)]
        pieces = pieces + [lax.ppermute(held, "pack", pairs) for held in pieces]
        xors = xors + [x ^ bit for x in xors]
        bit //= 2
    return pieces, xors


def local(
    hidden,
    first_keys,
    first_values,
    w_query,
    w_out,
    norm_gain,
    router_weight,
    route_list,
    pack_order,
    pattern,
):
    n_ctx = lax.axis_size("ctx")
    n_pack = lax.axis_size("pack")
    ctx = lax.axis_index("ctx")
    pack = lax.axis_index("pack")
    tok, width = hidden.shape
    span, part = first_keys.shape
    routed = route_list.shape[1]
    own = routed // n_pack
    cap = 3 * tok // 8
    group_width = part // GROUPS
    tall = group_width + TAIL
    ids = jnp.stack([ctx, pack]).astype(jnp.int32)
    whole = lambda shape: pl.BlockSpec(shape, lambda *_: (0,) * len(shape))
    in_hbm = pl.BlockSpec(memory_space=pltpu.HBM)
    bf16, f32 = jnp.bfloat16, jnp.float32
    shape_of = jax.ShapeDtypeStruct

    held = []
    for group in range(GROUPS):
        held.append(
            run(
                functools.partial(split_body, group),
                grid=(1,),
                scalars=0,
                in_specs=[in_hbm, in_hbm],
                out_specs=whole((2 * span, group_width)),
                out_shape=shape_of((2 * span, group_width), bf16),
                scratch=[pltpu.SemaphoreType.DMA((2,))],
                cost=cost_of(0, 8 * span * group_width),
            )(first_keys, first_values)
        )
    swap = [(c, c ^ 1) for c in range(n_ctx)]
    across = [lax.ppermute(kv, "ctx", swap) for kv in held]

    outgoing = run(
        pick_body,
        grid=(1,),
        scalars=1,
        in_specs=[whole((1, routed)), whole((tok, width))],
        out_specs=whole((cap, width)),
        out_shape=shape_of((cap, width), bf16),
        cost=cost_of(2 * cap * tok * width, 2 * tok * width * 2),
    )(ids, route_list, hidden)
    pieces, xors = gather_pack(outgoing, n_pack)

    picked = jnp.sum(
        jnp.where(
            pack_order[0][:, None] == jnp.arange(routed, dtype=jnp.int32)[None, :],
            route_list[0][None, :],
            0,
        ),
        axis=1,
    )
    position = picked + ctx * span
    half = HD // 2
    frequency = 10000.0 ** (-jnp.arange(half, dtype=f32) * 2.0 / HD)
    angle = position.astype(f32)[:, None] * frequency[None, :]
    cosine, sine = jnp.cos(angle), jnp.sin(angle)
    cosine = jnp.concatenate([cosine, cosine], axis=1)
    sine = jnp.concatenate([-sine, sine], axis=1)

    rows, gate, *queries = run(
        functools.partial(query_body, xors, tok, GROUPS),
        grid=(1,),
        scalars=1,
        in_specs=[whole((cap, width))] * n_pack
        + [
            whole((1, routed)),
            whole((1, routed)),
            whole((1, width)),
            whole((1, width)),
            whole((routed, HD)),
            whole((routed, HD)),
            in_hbm,
        ],
        out_specs=[whole((routed, width)), whole((routed, HD))]
        + [whole((routed, group_width))] * GROUPS,
        out_shape=[shape_of((routed, width), bf16), shape_of((routed, HD), f32)]
        + [shape_of((routed, group_width), bf16)] * GROUPS,
        scratch=[pltpu.VMEM((width, part), bf16), pltpu.SemaphoreType.DMA],
        cost=cost_of(2 * routed * width * (part + n_pack * cap), 6 * width * part),
        mib=32,
    )(
        ids,
        *pieces,
        route_list,
        pack_order,
        norm_gain.reshape(1, width),
        router_weight.reshape(1, width),
        cosine,
        sine,
        w_query,
    )

    w_in, _ = lax.optimization_barrier((w_out, pieces[1]))
    w_pieces, _ = gather_pack(w_in, n_pack)

    def attend(group, shift, query, use, prior=None):
        masked = shift == 0 and "own" in use
        given = [picked.reshape(1, routed)] if masked else []
        specs = [whole((1, routed))] if masked else []
        if prior is not None:
            given.append(prior)
            specs.append(whole((tall, routed)))
        arrays = [held[group] if kind == "own" else across[group] for kind in use]
        return run(
            functools.partial(attend_body, shift, use, prior is not None, n_ctx),
            grid=(1,),
            scalars=2,
            in_specs=specs
            + [whole((routed, group_width))]
            + [whole((2 * span, group_width))] * len(arrays),
            out_specs=whole((tall, routed)),
            out_shape=shape_of((tall, routed), bf16),
            scratch=[
                pltpu.VMEM((8, routed), f32),
                pltpu.VMEM((8, routed), f32),
                pltpu.VMEM((group_width, routed), f32),
            ],
            cost=cost_of(4 * len(use) * routed * span * group_width, 4 * span * group_width),
        )(ids, pattern, *given, query, *arrays)

    shifts = list(range(n_ctx // 2 - 1, 0, -1))
    attended = []
    for group in range(GROUPS):
        query = queries[group]
        first = attend(group, 0, query, ("own",))
        returned = []
        for shift in shifts:
            arrived = lax.ppermute(
                query, "ctx", [(c, c - 2 * shift) for c in range(2 * shift, n_ctx)]
            )
            if group < GROUPS - 1:
                partial = attend(group, shift, arrived, ("own", "other"))
            else:
                early = attend(group, shift, arrived, ("own",))
                partial = attend(group, shift, arrived, ("other",), early)
            returned.append(
                lax.ppermute(partial, "ctx", [(c, c + 2 * shift) for c in range(n_ctx - 2 * shift)])
            )
        second = attend(group, 0, query, ("other",), first)
        attended.append(
            run(
                functools.partial(merge_body, [0, *shifts]),
                grid=(1,),
                scalars=1,
                in_specs=[whole((tall, routed))] * (1 + len(shifts)),
                out_specs=whole((group_width, routed)),
                out_shape=shape_of((group_width, routed), bf16),
                cost=cost_of(8 * routed * group_width, 2 * tall * routed * (1 + len(shifts))),
            )(ids, second, *returned)
        )

    mixed = [gather_pack(value, n_pack)[0] for value in attended]

    def project_part(at, chosen, offset, prior):
        count = len(chosen)
        given = [] if prior is None else [prior]
        return run(
            functools.partial(partial_body, count, offset, prior is not None),
            grid=(1,),
            scalars=0,
            in_specs=[whole((group_width, routed))] * count
            + [whole((part, width))] * count
            + [whole((routed, width))] * len(given),
            out_specs=whole((routed, width)),
            out_shape=shape_of((routed, width), f32),
            cost=cost_of(2 * count * routed * group_width * width, 4 * routed * width),
        )(*[mixed[at][i] for i in chosen], *[w_pieces[i] for i in chosen], *given)

    total = None
    for group in range(GROUPS - 1):
        total = project_part(group, list(range(n_pack)), group * group_width, total)
    last = GROUPS - 1
    near = [i for i, x in enumerate(xors) if x < 2]
    distant = [i for i, x in enumerate(xors) if x >= 2]
    total = project_part(last, near, last * group_width, total)

    columns = width // 4
    hidden_out, packed = run(
        functools.partial(finish_body, len(distant), last * group_width),
        grid=(width // columns,),
        scalars=1,
        in_specs=[whole((group_width, routed))] * len(distant)
        + [whole((part, width))] * len(distant)
        + [
            whole((routed, width)),
            whole((routed, width)),
            whole((routed, HD)),
            whole((1, routed)),
            whole((tok, width)),
        ],
        out_specs=[
            pl.BlockSpec((tok, columns), lambda j, *_: (0, j)),
            pl.BlockSpec((own, columns), lambda j, *_: (0, j)),
        ],
        out_shape=[shape_of((tok, width), hidden.dtype), shape_of((own, width), hidden.dtype)],
        scratch=[pltpu.VMEM((routed, columns), bf16)],
        cost=cost_of(routed * width * width, 2 * width * width),
    )(
        ids,
        *[mixed[last][i] for i in distant],
        *[w_pieces[i] for i in distant],
        total,
        rows,
        gate,
        picked.reshape(1, routed),
        hidden,
    )
    return (hidden_out, packed)


def solution(mesh):
    return jax.shard_map(
        local,
        mesh=mesh,
        in_specs=(
            P(("ctx", "pack"), None),
            P("ctx", "pack"),
            P("ctx", "pack"),
            P(None, "pack"),
            P("pack", None),
            P(),
            P(),
            P("ctx", None),
            P("ctx", None),
            P(),
        ),
        out_specs=(P(("ctx", "pack"), None), P(("ctx", "pack"), None)),
        check_vma=False,
    )
```

```python
import functools
import math

import jax
import jax.numpy as jnp
import numpy as np
from jax import lax
from jax.experimental import pallas as pl
from jax.experimental.pallas import tpu as pltpu
from jax.sharding import PartitionSpec as P


HD = 128
EPS = 1e-06
NEG = -1e30
TAIL = 16
GROUPS = 2
SCALE = math.log2(math.e) / math.sqrt(HD)


def contract(left, right, left_dim, right_dim):
    return lax.dot_general(
        left, right, (((left_dim,), (right_dim,)), ((), ())), preferred_element_type=jnp.float32
    )


def run(body, *, grid, scalars, in_specs, out_specs, out_shape, scratch=(), cost=None, mib=16):
    kernel = call(body, grid, scalars, in_specs, out_specs, out_shape, scratch, cost, mib)

    return kernel


def call(body, grid, scalars, in_specs, out_specs, out_shape, scratch, cost, mib):
    return pl.pallas_call(
        body,
        grid_spec=pltpu.PrefetchScalarGridSpec(
            num_scalar_prefetch=scalars,
            grid=grid,
            in_specs=in_specs,
            out_specs=out_specs,
            scratch_shapes=list(scratch),
        ),
        out_shape=out_shape,
        cost_estimate=cost,
        compiler_params=pltpu.CompilerParams(vmem_limit_bytes=mib * 2**20),
    )


def cost_of(flops, moved, exps=0):
    return pl.CostEstimate(flops=int(flops), bytes_accessed=int(moved), transcendentals=int(exps))


def below(routes, bound):
    return jnp.sum(jnp.where(routes < bound, 1.0, 0.0), axis=1, keepdims=True).astype(jnp.int32)


def pick_body(ids, routes_ref, hidden_ref, out_ref):
    tok = hidden_ref.shape[0]
    cap = out_ref.shape[0]
    routed = routes_ref.shape[1]
    base = ids[1] * tok
    routes = routes_ref[...]
    token = lax.broadcasted_iota(jnp.int32, (tok, routed), 0) + base
    hit = jnp.where(routes == token, 1.0, 0.0).astype(jnp.bfloat16)
    entry = lax.broadcasted_iota(jnp.int32, (cap, routed), 1)
    slot = lax.broadcasted_iota(jnp.int32, (cap, routed), 0)
    choose = jnp.where(entry == slot + below(routes, base), 1.0, 0.0).astype(jnp.bfloat16)
    one_hot = contract(choose, hit, 1, 1).astype(jnp.bfloat16)
    out_ref[...] = contract(one_hot, hidden_ref[...], 1, 0).astype(out_ref.dtype)


def query_body(xors, tok, ids, *refs):
    count = len(xors)
    pieces = refs[:count]
    lists_ref, vectors_ref, cos_ref, sin_ref, wq_ref = refs[count : count + 5]
    rows_ref, gate_ref, query_ref = refs[count + 5 :]
    cap = pieces[0].shape[0]
    routed = lists_ref.shape[1]
    routes = lists_ref[0:1, :]
    order = lists_ref[1:2, :]
    entry = lax.broadcasted_iota(jnp.int32, (cap, routed), 0)
    rows = None
    for xor, piece in zip(xors, pieces):
        owner = ids[1] ^ xor
        listed = entry + below(routes, owner * tok)
        stop = below(routes, (owner + 1) * tok)
        one_hot = jnp.where((order == listed) & (listed < stop), 1.0, 0.0).astype(jnp.bfloat16)
        term = contract(one_hot, piece[...], 0, 0)
        rows = term if rows is None else rows + term
    rows_ref[...] = rows.astype(rows_ref.dtype)
    logit = jnp.sum(rows * vectors_ref[1:2, :], axis=1, keepdims=True)
    gate_ref[...] = jnp.broadcast_to(1.0 / (1.0 + jnp.exp(-logit)), gate_ref.shape)
    mean_square = jnp.mean(rows * rows, axis=1, keepdims=True)
    normed = (rows * lax.rsqrt(mean_square + EPS) * vectors_ref[0:1, :]).astype(jnp.bfloat16)
    projected = contract(normed, wq_ref[...], 1, 0)
    cosine = cos_ref[...]
    sine = sin_ref[...]
    for head in range(query_ref.shape[1] // HD):
        part = projected[:, head * HD : (head + 1) * HD]
        turned = part * cosine + pltpu.roll(part, HD // 2, 1) * sine
        query_ref[:, head * HD : (head + 1) * HD] = turned.astype(jnp.bfloat16)


def angle_body(span, ids, routes_ref, order_ref, gain_ref, router_ref, freq_ref, *out_refs):
    cos_ref, sin_ref, picked_ref, lists_ref, vectors_ref = out_refs
    routed = routes_ref.shape[1]
    routes = routes_ref[...].astype(jnp.float32)
    entry = lax.broadcasted_iota(jnp.int32, (routed, routed), 0)
    listed = jnp.transpose(jnp.broadcast_to(routes, (routed, routed)))
    picked = jnp.sum(jnp.where(order_ref[...] == entry, listed, 0.0), axis=0, keepdims=True)
    picked_ref[...] = picked.astype(jnp.int32)
    position = jnp.transpose(jnp.broadcast_to(picked, (HD, routed))) + (ids[0] * span).astype(
        jnp.float32
    )
    angle = position * freq_ref[...]
    cos_ref[...] = jnp.cos(angle)
    lane = lax.broadcasted_iota(jnp.int32, angle.shape, 1)
    sine = jnp.sin(angle)
    sin_ref[...] = jnp.where(lane < HD // 2, -sine, sine)
    lists_ref[0:1, :] = routes_ref[...]
    lists_ref[1:2, :] = order_ref[...]
    vectors_ref[0:1, :] = gain_ref[...]
    vectors_ref[1:2, :] = router_ref[...]


def copy_body(in_ref, out_ref):
    out_ref[...] = in_ref[...]


def split_body(keys_hbm, values_hbm, *refs):
    out_refs, sems = refs[:-1], refs[-1]
    loads = []
    for group, out_ref in enumerate(out_refs):
        span, width = out_ref.shape[0] // 2, out_ref.shape[1]
        for at, source in enumerate((keys_hbm, values_hbm)):
            load = pltpu.make_async_copy(
                source.at[:, pl.ds(group * width, width)],
                out_ref.at[pl.ds(at * span, span), :],
                sems.at[2 * group + at],
            )
            load.start()
            loads.append(load)
    for load in loads:
        load.wait()


def level_rows(part_ref, heads):
    tail = part_ref[heads * HD :, :].astype(jnp.float32)
    return [
        tail[head : head + 1] + tail[heads + head : heads + head + 1]
        + tail[2 * heads + head : 2 * heads + head + 1]
        for head in range(heads)
    ]


def attend_body(group, shift, use, prior, n_ctx, ids, pattern, *refs):
    masked_own = shift == 0 and "own" in use
    if masked_own:
        qpos_ref, refs = refs[0], refs[1:]
    if prior:
        prior_ref, refs = refs[0], refs[1:]
    q_ref, refs = refs[0], refs[1:]
    spans, refs = refs[: len(use)], refs[len(use) :]
    out_ref, m_ref, l_ref, acc_ref = refs
    span = spans[0].shape[0] // 2
    chunk = min(span, 1024)
    heads = spans[0].shape[1] // HD
    here = ids[0]
    source = here + 2 * shift
    row = jnp.minimum(source, n_ctx - 1)

    def attends(key_span):
        found = pattern[row, 0] == key_span
        for at in range(1, pattern.shape[1]):
            found = found | (pattern[row, at] == key_span)
        return found & (source < n_ctx) & (key_span < source)

    def block(kv_ref, masked, fresh):
        for at in range(0, span, chunk):
            for head in range(heads):
                cut = slice(head * HD, (head + 1) * HD)
                query = q_ref[:, (group * heads + head) * HD : (group * heads + head + 1) * HD]
                scores = contract(kv_ref[at : at + chunk, cut], query, 1, 1) * SCALE
                if masked:
                    kpos = lax.broadcasted_iota(jnp.int32, scores.shape, 0) + at
                    scores = jnp.where(kpos <= qpos_ref[...], scores, NEG)
                peak = jnp.max(scores, axis=0, keepdims=True)
                if not (fresh and at == 0):
                    former = m_ref[head : head + 1, :]
                    peak = jnp.maximum(former, peak)
                weights = jnp.exp2(scores - peak)
                total = jnp.sum(weights, axis=0, keepdims=True)
                value = contract(
                    kv_ref[span + at : span + at + chunk, cut], weights.astype(jnp.bfloat16), 0, 0
                )
                if not (fresh and at == 0):
                    fade = jnp.exp2(former - peak)
                    total = l_ref[head : head + 1, :] * fade + total
                    value = acc_ref[cut, :] * fade + value
                m_ref[head : head + 1, :] = peak
                l_ref[head : head + 1, :] = total
                acc_ref[cut, :] = value

    if masked_own:
        block(spans[0], True, True)
    else:
        if prior:
            for head, level in enumerate(level_rows(prior_ref, heads)):
                m_ref[head : head + 1, :] = level
                l_ref[head : head + 1, :] = jnp.where(level > 0.5 * NEG, 1.0, 0.0)
            acc_ref[...] = prior_ref[: heads * HD, :].astype(jnp.float32)
        else:
            m_ref[...] = jnp.full_like(m_ref, NEG)
            l_ref[...] = jnp.zeros_like(l_ref)
            acc_ref[...] = jnp.zeros_like(acc_ref)
        for kind, kv_ref in zip(use, spans):
            key_span = here if kind == "own" else here ^ 1
            pl.when(attends(key_span))(functools.partial(block, kv_ref, False, False))

    index = lax.broadcasted_iota(jnp.int32, (TAIL, out_ref.shape[1]), 0)
    tail = jnp.zeros(index.shape, jnp.float32)
    for head in range(heads):
        cut = slice(head * HD, (head + 1) * HD)
        total = l_ref[head : head + 1, :]
        some = total > 0.0
        safe = jnp.where(some, total, 1.0)
        out_ref[cut, :] = (acc_ref[cut, :] * (1.0 / safe)).astype(out_ref.dtype)
        rest = jnp.where(some, m_ref[head : head + 1, :] + jnp.log2(safe), NEG)
        for digit in range(3):
            value = rest.astype(jnp.bfloat16).astype(jnp.float32)
            tail = jnp.where(index == digit * heads + head, value, tail)
            rest = rest - value
    out_ref[heads * HD :, :] = tail.astype(out_ref.dtype)


def merge_body(shifts, ids, *refs):
    parts, out_ref = refs[:-1], refs[-1]
    heads = out_ref.shape[0] // HD
    levels = []
    for shift, part in zip(shifts, parts):
        rows = level_rows(part, heads)
        if shift:
            rows = [jnp.where(ids[0] >= 2 * shift, row, NEG) for row in rows]
        levels.append(rows)
    for head in range(heads):
        cut = slice(head * HD, (head + 1) * HD)
        mine = [rows[head] for rows in levels]
        peak = functools.reduce(jnp.maximum, mine)
        weights = [jnp.exp2(level - peak) for level in mine]
        inverse = 1.0 / functools.reduce(lambda a, b: a + b, weights)
        total = None
        for weight, part in zip(weights, parts):
            term = part[cut, :].astype(jnp.float32) * (weight * inverse)
            total = term if total is None else total + term
        out_ref[cut, :] = total.astype(out_ref.dtype)


def project(attended, weights, offset, columns):
    part = attended[0].shape[0]
    mixed = None
    for rows, weight in zip(attended, weights):
        term = contract(rows[...], weight[offset : offset + part, columns], 0, 0)
        mixed = term if mixed is None else mixed + term
    return mixed


def partial_body(count, offset, prior, *refs):
    attended, weights = refs[:count], refs[count : 2 * count]
    out_ref = refs[-1]
    width = out_ref.shape[1]
    step = min(512, width)
    for at in range(0, width, step):
        columns = slice(at, at + step)
        mixed = project(attended, weights, offset, columns)
        if prior:
            mixed = mixed + refs[2 * count][:, columns]
        out_ref[:, columns] = mixed


def finish_body(count, offset, ids, *refs):
    attended, weights = refs[:count], refs[count : 2 * count]
    sum_ref, rows_ref, gate_ref, picked_ref, hidden_ref = refs[2 * count : 2 * count + 5]
    hidden_out, packed_out, new_ref = refs[2 * count + 5 :]
    tok = hidden_ref.shape[0]
    routed = rows_ref.shape[0]
    own = packed_out.shape[0]
    step = hidden_out.shape[1]
    columns = pl.ds(pl.multiple_of(pl.program_id(0) * step, step), step)
    token = lax.broadcasted_iota(jnp.int32, (tok, routed), 0) + ids[1] * tok
    place = jnp.where(picked_ref[...] == token, 1.0, 0.0)
    filled = jnp.sum(place, axis=1, keepdims=True) > 0.0
    mixed = project(attended, weights, offset, columns) + sum_ref[:, columns]
    new = rows_ref[:, columns].astype(jnp.float32) + gate_ref[:, 0:1] * mixed
    new_ref[...] = new.astype(new_ref.dtype)
    packed_out[...] = new_ref[pl.ds(pl.multiple_of(ids[1] * own, own), own), :]
    moved = contract(place.astype(jnp.bfloat16), new_ref[...], 1, 0)
    hidden_out[...] = jnp.where(
        filled, moved, hidden_ref[:, columns].astype(jnp.float32)
    ).astype(hidden_out.dtype)


def gather_pack(piece, n_pack):
    pieces, xors = [piece], [0]
    bit = n_pack // 2
    while bit:
        pairs = [(p, p ^ bit) for p in range(n_pack)]
        pieces = pieces + [lax.ppermute(held, "pack", pairs) for held in pieces]
        xors = xors + [x ^ bit for x in xors]
        bit //= 2
    return pieces, xors


def local(
    hidden,
    first_keys,
    first_values,
    w_query,
    w_out,
    norm_gain,
    router_weight,
    route_list,
    pack_order,
    pattern,
):
    n_ctx = lax.axis_size("ctx")
    n_pack = lax.axis_size("pack")
    ctx = lax.axis_index("ctx")
    pack = lax.axis_index("pack")
    tok, width = hidden.shape
    span, part = first_keys.shape
    routed = route_list.shape[1]
    own = routed // n_pack
    cap = 3 * tok // 8
    group_width = part // GROUPS
    tall = group_width + TAIL
    ids = jnp.stack([ctx, pack]).astype(jnp.int32)
    whole = lambda shape: pl.BlockSpec(shape, lambda *_: (0,) * len(shape))
    in_hbm = pl.BlockSpec(memory_space=pltpu.HBM)
    bf16, f32 = jnp.bfloat16, jnp.float32
    shape_of = jax.ShapeDtypeStruct

    held = run(
        split_body,
        grid=(1,),
        scalars=0,
        in_specs=[in_hbm, in_hbm],
        out_specs=[whole((2 * span, group_width))] * GROUPS,
        out_shape=[shape_of((2 * span, group_width), bf16)] * GROUPS,
        scratch=[pltpu.SemaphoreType.DMA((2 * GROUPS,))],
        cost=cost_of(0, 8 * span * part),
        mib=8,
    )(
        pltpu.with_memory_space_constraint(first_keys, pltpu.HBM),
        pltpu.with_memory_space_constraint(first_values, pltpu.HBM),
    )
    swap = [(c, c ^ 1) for c in range(n_ctx)]
    across = [lax.ppermute(kv, "ctx", swap) for kv in held]

    outgoing = run(
        pick_body,
        grid=(1,),
        scalars=1,
        in_specs=[whole((1, routed)), whole((tok, width))],
        out_specs=whole((cap, width)),
        out_shape=shape_of((cap, width), bf16),
        cost=cost_of(2 * cap * tok * width, 2 * tok * width * 2),
    )(ids, route_list, hidden)
    pieces, xors = gather_pack(outgoing, n_pack)

    half = 10000.0 ** (-np.arange(HD // 2, dtype=np.float32) * np.float32(2.0) / np.float32(HD))
    frequency = np.concatenate([half, half]).astype(np.float32)[None, :]
    cosine, sine, picked, lists, vectors = run(
        functools.partial(angle_body, span),
        grid=(1,),
        scalars=1,
        in_specs=[whole((1, routed))] * 2 + [whole((1, width))] * 2 + [whole((1, HD))],
        out_specs=[whole((routed, HD))] * 2
        + [whole((1, routed)), whole((2, routed)), whole((2, width))],
        out_shape=[shape_of((routed, HD), f32)] * 2
        + [
            shape_of((1, routed), jnp.int32),
            shape_of((2, routed), jnp.int32),
            shape_of((2, width), f32),
        ],
        cost=cost_of(100 * routed * HD, 8 * routed * HD),
        mib=8,
    )(
        ids,
        route_list,
        pack_order,
        norm_gain.reshape(1, width),
        router_weight.reshape(1, width),
        jnp.asarray(frequency),
    )

    fetched = run(
        copy_body,
        grid=(1,),
        scalars=0,
        in_specs=[whole((width, part))],
        out_specs=whole((width, part)),
        out_shape=shape_of((width, part), bf16),
        cost=cost_of(0, 4 * width * part),
        mib=8,
    )(w_query)

    rows, gate, queries = run(
        functools.partial(query_body, xors, tok),
        grid=(1,),
        scalars=1,
        in_specs=[whole((cap, width))] * n_pack
        + [
            whole((2, routed)),
            whole((2, width)),
            whole((routed, HD)),
            whole((routed, HD)),
            whole((width, part)),
        ],
        out_specs=[whole((routed, width)), whole((routed, HD))]
        + [whole((routed, part))],
        out_shape=[shape_of((routed, width), bf16), shape_of((routed, HD), f32)]
        + [shape_of((routed, part), bf16)],
        cost=cost_of(2 * routed * width * (part + n_pack * cap), 6 * width * part),
        mib=20,
    )(
        ids,
        *pieces,
        lists,
        vectors,
        cosine,
        sine,
        fetched,
    )

    w_in, _ = lax.optimization_barrier((w_out, pieces[1]))
    w_pieces, _ = gather_pack(w_in, n_pack)

    def attend(group, shift, query, use, prior=None):
        masked = shift == 0 and "own" in use
        given = [picked] if masked else []
        specs = [whole((1, routed))] if masked else []
        if prior is not None:
            given.append(prior)
            specs.append(whole((tall, routed)))
        arrays = [held[group] if kind == "own" else across[group] for kind in use]
        return run(
            functools.partial(attend_body, group, shift, use, prior is not None, n_ctx),
            grid=(1,),
            scalars=2,
            in_specs=specs
            + [whole((routed, part))]
            + [whole((2 * span, group_width))] * len(arrays),
            out_specs=whole((tall, routed)),
            out_shape=shape_of((tall, routed), bf16),
            scratch=[
                pltpu.VMEM((8, routed), f32),
                pltpu.VMEM((8, routed), f32),
                pltpu.VMEM((group_width, routed), f32),
            ],
            cost=cost_of(4 * len(use) * routed * span * group_width, 4 * span * group_width),
        )(ids, pattern, *given, query, *arrays)

    shifts = list(range(n_ctx // 2 - 1, 0, -1))
    arrived = {
        shift: lax.ppermute(queries, "ctx", [(c, c - 2 * shift) for c in range(2 * shift, n_ctx)])
        for shift in shifts
    }
    attended = []
    for group in range(GROUPS):
        first = attend(group, 0, queries, ("own",))
        returned = []
        for shift in shifts:
            if group < GROUPS - 1:
                partial = attend(group, shift, arrived[shift], ("own", "other"))
            else:
                early = attend(group, shift, arrived[shift], ("own",))
                partial = attend(group, shift, arrived[shift], ("other",), early)
            returned.append(
                lax.ppermute(partial, "ctx", [(c, c + 2 * shift) for c in range(n_ctx - 2 * shift)])
            )
        second = attend(group, 0, queries, ("other",), first)
        attended.append(
            run(
                functools.partial(merge_body, [0, *shifts]),
                grid=(1,),
                scalars=1,
                in_specs=[whole((tall, routed))] * (1 + len(shifts)),
                out_specs=whole((group_width, routed)),
                out_shape=shape_of((group_width, routed), bf16),
                cost=cost_of(8 * routed * group_width, 2 * tall * routed * (1 + len(shifts))),
            )(ids, second, *returned)
        )

    mixed = [gather_pack(value, n_pack)[0] for value in attended]

    def project_part(at, chosen, offset, prior):
        count = len(chosen)
        given = [] if prior is None else [prior]
        return run(
            functools.partial(partial_body, count, offset, prior is not None),
            grid=(1,),
            scalars=0,
            in_specs=[whole((group_width, routed))] * count
            + [whole((part, width))] * count
            + [whole((routed, width))] * len(given),
            out_specs=whole((routed, width)),
            out_shape=shape_of((routed, width), f32),
            cost=cost_of(2 * count * routed * group_width * width, 4 * routed * width),
        )(*[mixed[at][i] for i in chosen], *[w_pieces[i] for i in chosen], *given)

    total = None
    for group in range(GROUPS - 1):
        total = project_part(group, list(range(n_pack)), group * group_width, total)
    last = GROUPS - 1
    near = [i for i, x in enumerate(xors) if x < 2]
    distant = [i for i, x in enumerate(xors) if x >= 2]
    total = project_part(last, near, last * group_width, total)

    columns = width // 4
    hidden_out, packed = run(
        functools.partial(finish_body, len(distant), last * group_width),
        grid=(width // columns,),
        scalars=1,
        in_specs=[whole((group_width, routed))] * len(distant)
        + [whole((part, width))] * len(distant)
        + [
            whole((routed, width)),
            whole((routed, width)),
            whole((routed, HD)),
            whole((1, routed)),
            whole((tok, width)),
        ],
        out_specs=[
            pl.BlockSpec((tok, columns), lambda j, *_: (0, j)),
            pl.BlockSpec((own, columns), lambda j, *_: (0, j)),
        ],
        out_shape=[shape_of((tok, width), hidden.dtype), shape_of((own, width), hidden.dtype)],
        scratch=[pltpu.VMEM((routed, columns), bf16)],
        cost=cost_of(routed * width * width, 2 * width * width),
    )(
        ids,
        *[mixed[last][i] for i in distant],
        *[w_pieces[i] for i in distant],
        total,
        rows,
        gate,
        picked,
        hidden,
    )
    return (hidden_out, packed)


def solution(mesh):
    return jax.shard_map(
        local,
        mesh=mesh,
        in_specs=(
            P(("ctx", "pack"), None),
            P("ctx", "pack"),
            P("ctx", "pack"),
            P(None, "pack"),
            P("pack", None),
            P(),
            P(),
            P("ctx", None),
            P("ctx", None),
            P(),
        ),
        out_specs=(P(("ctx", "pack"), None), P(("ctx", "pack"), None)),
        check_vma=False,
    )
```
